32 devices in a mesh: groups: 2 (over y), choice: 16 (over z, x, core).
Axes of the slice: x: 2, y: 2, z: 4, core: 2. Of those that a mesh axis runs over, the one named last changes fastest.
Arguments:
- transitions: bfloat16 [4096, 6, 128, 128], P('choice'), may hold values from -0.21875 to 0.21875
- col_block: int32 [4096, 6], P('choice'), may hold values from 0 to 63
- reward_class: int32 [4, 4096, 128], P(None, 'choice'), may hold values from 0 to 127
- reward_table: bfloat16 [4, 128, 256], P(None, None, 'groups'), parts along dimension 2, may hold values from -6 to 310
- terminal: bfloat16 [8192, 256], P('choice', 'groups'), parts along dimension 1, may hold values from -6 to 6
Outputs:
- values: float32 [8192, 256], P('choice', 'groups'), parts along dimension 1
The draws below stay inside these ranges and needn't reach their ends.
There are 2 independent parts, one for each index of `groups`. The reference program is written for one: setup_inputs(seed, part) draws one part's arguments, and reference() takes and returns one part's arrays. A program takes and returns all parts, laid end to end along the dimension named above; an argument that names none is the same for every part. Nothing has to cross between parts.
All inputs are finite; a program needn't handle non-finite values.
Results may differ from the reference program's by a relative error of at most 0.0013.
Values may be sent and summed in bfloat16 or wider, within the bound.
A program may use at most 256 MiB of HBM per device.

```python
import jax
import jax.numpy as jnp
from jax import lax

NB = 64
BLK = 128
J = 64
K = 6
R = 128
P_SIZE = 128
AGES = 4
STATES = 8192
PAIRS = 4096


def draw_reward_table(key, part):
    base = 1.5 * jax.random.normal(jax.random.fold_in(key, 11), (AGES, R, P_SIZE), jnp.float32)
    base = jnp.clip(base, -6.0, 6.0)
    return base.astype(jnp.bfloat16)


def plant(values, rng, least, high):
    longest = values.shape.index(max(values.shape))
    spots = []
    for shift in (0, 1):
        where = [jax.random.randint(jax.random.fold_in(rng, axis), (), 0, length) for axis, length in enumerate(values.shape)]
        where[longest] = (where[longest] + shift) % values.shape[longest]
        spots.append(tuple(where))
    return values.at[spots[0]].set(least).at[spots[1]].set(high)


def shard_levels(key, extent, shards, low, largest):
    gain = 1.0
    for dim, shards_of in shards:
        draws = jax.random.uniform(jax.random.fold_in(jax.random.fold_in(key, 6), dim), (shards_of,), jnp.float32, low / len(shards), largest / len(shards))
        gain = gain * jnp.repeat(jnp.exp(draws), extent[dim] // shards_of).reshape((-1,) + (1,) * (len(extent) - 1 - dim))
    return gain


def centred(rng, extent, spread, most, pieces=(), kind=jnp.bfloat16):
    result = jax.random.normal(rng, extent, jnp.float32) * spread
    if len(pieces) > 0:
        result = shard_levels(rng, extent, pieces, -0.22, 0.18) * result
    return jnp.clip(result, min=-most, max=most).astype(kind)


def setup_inputs(seed: int = 0, part: int = 0) -> dict:
    keys = jax.random.split(jax.random.key(seed), 6)
    part_splits = jax.random.split(jax.random.fold_in(keys[5], part), 6)
    transitions = centred(keys[0], (PAIRS, K, BLK, BLK), (K * BLK) ** -0.5, 0.21875, ((0, 16),))
    col_block = plant(jax.random.randint(keys[1], (PAIRS, K), 0, NB), jax.random.fold_in(keys[1], 1), 0, NB - 1).astype(jnp.int32)
    reward_class = plant(jax.random.randint(keys[2], (AGES, PAIRS, BLK), 0, R), jax.random.fold_in(keys[2], 1), 0, R - 1).astype(jnp.int32)
    reward_table = draw_reward_table(jax.random.fold_in(jax.random.fold_in(keys[5], part), 71), part)
    terminal = centred(part_splits[4], (STATES, P_SIZE), 1.0, 6.0, ((0, 16),))
    return {"transitions": transitions, "col_block": col_block, "reward_class": reward_class, "reward_table": reward_table, "terminal": terminal}


def reference(transitions, col_block, reward_class, reward_table, terminal):
    next_values = terminal
    current = jnp.zeros((STATES, P_SIZE), jnp.float32)
    for age_index in range(AGES - 1, -1, -1):
        reward_rows = reward_table[age_index].astype(jnp.float32)
        value_blocks = next_values.astype(jnp.float32).reshape(NB, BLK, P_SIZE)
        classes_all = reward_class[age_index]

        def one_row(row_block):
            start = (row_block * J).astype(jnp.int32)
            kernel = lax.dynamic_slice_in_dim(transitions, start, J, 0).astype(jnp.float32)
            column_ids = lax.dynamic_slice_in_dim(col_block, start, J, 0)
            picked = value_blocks[column_ids]
            expected = jnp.einsum("jkab,jkbq->jaq", kernel, picked, precision=lax.Precision.HIGHEST)
            classes = lax.dynamic_slice_in_dim(classes_all, start, J, 0)
            scores = expected + reward_rows[classes]
            highest = jnp.max(scores, axis=0)
            return highest + jnp.log(jnp.sum(jnp.exp(scores - highest[None]), axis=0))

        current = lax.map(one_row, jnp.arange(NB, dtype=jnp.int32)).reshape(STATES, P_SIZE)
        if age_index > 0:
            next_values = current.astype(jnp.bfloat16)
    return current
```

```python
import functools

import jax
import jax.numpy as jnp
from jax import lax
from jax.experimental import pallas as pl
from jax.experimental.pallas import tpu as pltpu
from jax.sharding import PartitionSpec as P

J = 64
AGES = 4
STATES = 8192


def partner(array, axis, apart):
    return lax.ppermute(array, axis, [(i, i ^ 1 << apart) for i in range(lax.axis_size(axis))])


def combine(earlier, later):
    highest = jnp.maximum(earlier[0], later[0])
    totals = earlier[1] * jnp.exp(earlier[0] - highest) + later[1] * jnp.exp(later[0] - highest)
    return (highest, totals)


def choice_partials(transitions, col_block, classes, reward_rows, next_values):
    pair_count = transitions.shape[0]
    block_rows = transitions.shape[2]
    columns = next_values.shape[1]
    stacked = next_values.reshape(STATES // block_rows, block_rows, columns)
    picked = jnp.take(stacked, col_block, axis=0)
    expected = jnp.einsum("pkab,pkbq->paq", transitions, picked, preferred_element_type=jnp.float32)
    onehot = (classes[:, :, None] == jnp.arange(reward_rows.shape[0], dtype=jnp.int32)).astype(
        jnp.bfloat16
    )
    reward = jnp.einsum("pbr,rq->pbq", onehot, reward_rows, preferred_element_type=jnp.float32)
    scores = expected + reward
    inner_count = min(J, pair_count)
    grouped = scores.reshape(pair_count // inner_count, inner_count, block_rows, columns)
    highest = jnp.max(grouped, axis=1)
    totals = jnp.sum(jnp.exp(grouped - highest[:, None]), axis=1)
    return (highest.reshape(-1, columns), totals.reshape(-1, columns))


def shards_split(transitions, col_block, reward_class, reward_table, terminal):
    devices = lax.axis_size("choice")
    pair_count = transitions.shape[0]
    inner_count = min(J, pair_count)
    group_size = J // inner_count
    swap_count = group_size.bit_length() - 1
    member_index = lax.axis_index("choice") % group_size
    share_rows = STATES // devices
    next_values = lax.all_gather(terminal, "choice", axis=0, tiled=True)
    result = None
    for age_index in range(AGES - 1, -1, -1):
        highest, totals = choice_partials(
            transitions, col_block, reward_class[age_index], reward_table[age_index], next_values
        )
        for bit_index in range(swap_count):
            incoming = partner((highest, totals), "choice", bit_index)
            highest, totals = combine((highest, totals), incoming)
        block_values = highest + jnp.log(totals)
        if age_index > 0:
            gathered = lax.all_gather(
                block_values.astype(jnp.bfloat16), "choice", axis=0, tiled=True
            )
            spread = gathered.astype(jnp.float32).reshape(
                devices // group_size, group_size, block_values.shape[0], block_values.shape[1]
            )
            next_values = (
                jnp.mean(spread, axis=1).astype(jnp.bfloat16).reshape(STATES, block_values.shape[1])
            )
        else:
            result = lax.dynamic_slice_in_dim(
                block_values, member_index * share_rows, share_rows, 0
            )
    return result


CHUNK = 8
MESH = pl.DeviceIdType.MESH


def chunk_scores(first, cols_ref, trans_ref, classes, table, load_block, scores_ref):
    size = trans_ref.shape[2]
    types = table.shape[0]
    depth = trans_ref.shape[1]
    kinds = lax.broadcasted_iota(jnp.int32, (types, size), 0)
    for i in range(CHUNK):
        blocks = [load_block(cols_ref[(first + i) * depth + k]) for k in range(depth)]
        left = jnp.concatenate([trans_ref[i, k] for k in range(depth)], axis=1)
        right = jnp.concatenate(blocks, axis=0)
        onehot = jnp.where(classes[i : i + 1, :] == kinds, 1.0, 0.0).astype(jnp.bfloat16)
        scores_ref[i] = jnp.dot(
            left, right, preferred_element_type=jnp.float32
        ) + lax.dot_general(
            onehot, table, (((0,), (0,)), ((), ())), preferred_element_type=jnp.float32
        )


def fold(scores_ref, high_ref, total_ref):
    before = high_ref[...]
    high = before
    for i in range(CHUNK):
        high = jnp.maximum(high, scores_ref[i])
    total = total_ref[...] * jnp.exp(before - high)
    for i in range(CHUNK):
        total = total + jnp.exp(scores_ref[i] - high)
    high_ref[...] = high
    total_ref[...] = total


def age_kernel(cols_ref, trans_ref, class_ref, table_ref, value_ref, out_ref, scores_ref, high_ref, total_ref):
    row, step = pl.program_id(0), pl.program_id(1)
    steps = pl.num_programs(1)

    @pl.when(step == 0)
    def _():
        high_ref[...] = jnp.full_like(high_ref, -jnp.inf)
        total_ref[...] = jnp.zeros_like(total_ref)

    chunk_scores(
        (row * steps + step) * CHUNK, cols_ref, trans_ref, class_ref[0], table_ref[0],
        lambda c: value_ref[c], scores_ref,
    )
    fold(scores_ref, high_ref, total_ref)

    @pl.when(step == steps - 1)
    def _():
        out_ref[0] = (high_ref[...] + jnp.log(total_ref[...])).astype(out_ref.dtype)


def one_age(age, cols, transitions, reward_class, reward_table, values, kind):
    pairs, depth, size, _ = transitions.shape
    types, columns = reward_table.shape[1:]
    rows, steps = pairs // J, J // CHUNK
    return pl.pallas_call(
        age_kernel,
        out_shape=jax.ShapeDtypeStruct((rows, size, columns), kind),
        grid_spec=pltpu.PrefetchScalarGridSpec(
            num_scalar_prefetch=1,
            grid=(rows, steps),
            in_specs=[
                pl.BlockSpec((CHUNK, depth, size, size), lambda r, s, c: (r * steps + s, 0, 0, 0)),
                pl.BlockSpec((1, CHUNK, size), lambda r, s, c: (age, r * steps + s, 0)),
                pl.BlockSpec((1, types, columns), lambda r, s, c: (age, 0, 0)),
                pl.BlockSpec(memory_space=pltpu.VMEM),
            ],
            out_specs=pl.BlockSpec((1, size, columns), lambda r, s, c: (r, 0, 0)),
            scratch_shapes=[
                pltpu.VMEM((CHUNK, size, columns), jnp.float32),
                pltpu.VMEM((size, columns), jnp.float32),
                pltpu.VMEM((size, columns), jnp.float32),
            ],
        ),
        cost_estimate=pl.CostEstimate(
            flops=2 * pairs * (depth * size + types) * size * columns,
            bytes_accessed=transitions.size * 2,
            transcendentals=pairs * size * columns,
        ),
    )(cols, transitions, reward_class, reward_table, values)


class Spread:
    def __init__(self, values, send, recv):
        self.values, self.send, self.recv = values, send, recv
        devices = lax.axis_size("choice")
        self.group = lax.axis_index("groups")
        self.me = lax.axis_index("choice")
        self.core, self.x, self.z = self.me % 2, (self.me // 2) % 2, self.me // 4
        self.depth = devices // 4
        self.across = self.place(self.z, 1 - self.x, self.core)
        self.beside = self.place(self.z, self.x, 1 - self.core)
        self.mates = [
            self.place((self.z + d) % self.depth, self.x, self.core) for d in range(1, self.depth)
        ]

    def place(self, z, x, core):
        return z * 4 + x * 2 + core

    def copy(self, way, rows, b, origin, target, source=None):
        block = self.values.at[origin * rows + b]
        return pltpu.make_async_remote_copy(
            src_ref=block if source is None else source,
            dst_ref=block,
            send_sem=self.send.at[b, way],
            recv_sem=self.recv.at[b, origin],
            device_id=(self.group, target),
            device_id_type=MESH,
        )

    def greet(self):
        barrier = pltpu.get_barrier_semaphore()
        near = self.mates + [self.across, self.beside]
        for target in near:
            pl.semaphore_signal(barrier, inc=1, device_id=(self.group, target), device_id_type=MESH)
        pl.semaphore_wait(barrier, len(near))

    def own(self, rows, b, source=None):
        d = self.depth
        out = [self.copy(i, rows, b, self.me, t, source) for i, t in enumerate(self.mates)]
        out.append(self.copy(d - 1, rows, b, self.me, self.across, source))
        out.append(self.copy(d, rows, b, self.me, self.beside, source))
        return out

    def along(self, rows, b):
        d = self.depth
        out = []
        for i, origin in enumerate(self.mates):
            out.append(self.copy(d + 1 + 2 * i, rows, b, origin, self.across))
            out.append(self.copy(d + 2 + 2 * i, rows, b, origin, self.beside))
        return out

    def over(self, rows, b):
        d = self.depth
        return [
            self.copy(3 * d - 1 + i, rows, b, self.place((self.z + i) % d, 1 - self.x, self.core), self.beside)
            for i in range(d)
        ]

    def last(self, rows, b):
        return [
            self.copy(0, rows, b, self.place((self.z + i) % self.depth, x, 1 - self.core), self.beside)
            for i in range(self.depth)
            for x in (0, 1)
        ]

    def start_own(self, rows, b, source=None):
        for c in self.own(rows, b, source):
            c.start()

    def start_along(self, rows, b):
        out = self.along(rows, b)
        for i in range(len(self.mates)):
            out[2 * i].wait_recv()
            out[2 * i].start()
            out[2 * i + 1].start()

    def start_over(self, rows, b):
        for c in self.over(rows, b):
            c.wait_recv()
            c.start()

    def finish(self, rows, b):
        for c in self.last(rows, b):
            c.wait_recv()

    def drain(self, rows, b):
        for c in self.own(rows, b) + self.along(rows, b) + self.over(rows, b):
            c.wait_send()


def ways(devices):
    return 4 * (devices // 4) - 1


def gather_kernel(own_ref, out_ref, send, recv, local):
    rows = own_ref.shape[0]
    spread = Spread(out_ref, send, recv)
    keep = pltpu.make_async_copy(own_ref, out_ref.at[pl.ds(spread.me * rows, rows)], local)
    keep.start()
    spread.greet()
    for b in range(rows):
        spread.start_own(rows, b, own_ref.at[b])
    for b in range(rows):
        spread.start_along(rows, b)
    for b in range(rows):
        spread.start_over(rows, b)
    for b in range(rows):
        spread.finish(rows, b)
    for b in range(rows):
        spread.drain(rows, b)
    keep.wait()


def gather(own):
    devices = lax.axis_size("choice")
    rows, size, columns = own.shape
    return pl.pallas_call(
        gather_kernel,
        out_shape=jax.ShapeDtypeStruct((rows * devices, size, columns), own.dtype),
        in_specs=[pl.BlockSpec(memory_space=pltpu.VMEM)],
        out_specs=pl.BlockSpec(memory_space=pltpu.VMEM),
        scratch_shapes=[
            pltpu.SemaphoreType.DMA((rows, ways(devices))),
            pltpu.SemaphoreType.DMA((rows, devices)),
            pltpu.SemaphoreType.DMA,
        ],
        compiler_params=pltpu.CompilerParams(collective_id=0, has_side_effects=True),
    )(own)


def shards_whole(transitions, col_block, reward_class, reward_table, terminal):
    size = transitions.shape[2]
    cols = col_block.reshape(-1)
    values = terminal.reshape(terminal.shape[0] // size, size, terminal.shape[1])
    for age in range(AGES - 1, -1, -1):
        kind = jnp.bfloat16 if age > 0 else jnp.float32
        values = one_age(age, cols, transitions, reward_class, reward_table, gather(values), kind)
    return values.reshape(terminal.shape)


def shards(transitions, col_block, reward_class, reward_table, terminal):
    whole = transitions.shape[0] % J == 0 and lax.axis_size("choice") % 4 == 0
    body = shards_whole if whole else shards_split
    return body(transitions, col_block, reward_class, reward_table, terminal)


def solution(mesh):
    return jax.shard_map(
        shards,
        mesh=mesh,
        in_specs=(
            P("choice", None, None, None),
            P("choice", None),
            P(None, "choice", None),
            P(None, None, "groups"),
            P("choice", "groups"),
        ),
        out_specs=P("choice", "groups"),
        check_vma=False,
    )
```
